32 devices in a mesh: groups: 2 (over x), tgt: 16 (over z, y, core).
Axes of the slice: x: 2, y: 2, z: 4, core: 2. Of those that a mesh axis runs over, the one named last changes fastest.
Arguments:
- target_features: bfloat16 [32768, 1024], P(('groups', 'tgt')), parts along dimension 0, may hold values from -16 to 16
- source_features: bfloat16 [2048, 1024], P(('groups', 'tgt')), parts along dimension 0, may hold values from -16 to 16
- vectors: bfloat16 [2048, 128], P(('groups', 'tgt')), parts along dimension 0, may hold values from -6 to 6
- current: float32 [32768, 128], P(('groups', 'tgt')), parts along dimension 0, may hold values from -6 to 6
- previous: float32 [32768, 128], P(('groups', 'tgt')), parts along dimension 0, may hold values from -100 to 100
Outputs:
- filtered: float32 [32768, 128], P(('groups', 'tgt')), parts along dimension 0
The draws below stay inside these ranges and needn't reach their ends.
There are 2 independent parts, one for each index of `groups`. The reference program is written for one: setup_inputs(seed, part) draws one part's arguments, and reference() takes and returns one part's arrays. A program takes and returns all parts, laid end to end along the dimension named above; each array names one. Nothing has to cross between parts.
All inputs are finite; a program needn't handle non-finite values.
Results may differ from the reference program's by a relative error of at most 0.002.
Values may be sent and summed in bfloat16 or wider, within the bound.
A program may use at most 128 MiB of HBM per device.

```python
import math
import jax
import jax.numpy as jnp
from jax import lax

D = 1024
COLS = 128
TGT_DEV = 1024
TARGETS = 16384
SOURCES = 1024


def features_pair(key):
    source = jnp.clip(jax.random.normal(jax.random.fold_in(key, 11), (SOURCES, D), jnp.float32), -6.0, 6.0)
    target = jnp.clip(jax.random.normal(jax.random.fold_in(key, 12), (TARGETS, D), jnp.float32), -6.0, 6.0)
    return (target, source)


def draw_target_features(key, part):
    return features_pair(key)[0].astype(jnp.bfloat16)


def draw_source_features(key, part):
    return features_pair(key)[1].astype(jnp.bfloat16)


def draw_previous(key, part):
    base = jnp.clip(jax.random.normal(jax.random.fold_in(key, 20), (TARGETS, COLS), jnp.float32), -6.0, 6.0)
    ramp = jnp.arange(TARGETS, dtype=jnp.float32) / max(TARGETS - 1, 1)
    row_scale = 0.1 * (1.0 + 2.0 * ramp) * jnp.exp(math.log(10.0) * jax.random.uniform(jax.random.fold_in(key, 21), (TARGETS,), jnp.float32))
    col_scale = 0.3 * jnp.exp(math.log(10.0) * jax.random.uniform(jax.random.fold_in(key, 22), (COLS,), jnp.float32))
    return base * row_scale[:, None] * col_scale[None, :]


def steps_of(key, dims, split, least, largest):
    level, own = 1.0, jax.random.fold_in(key, 6)
    for axis_at, blocks in split:
        draws = jnp.exp(jax.random.uniform(jax.random.fold_in(own, axis_at), (blocks,), jnp.float32, least / len(split), largest / len(split)))
        level = level * jnp.repeat(draws, dims[axis_at] // blocks).reshape([-1 if axis == axis_at else 1 for axis in range(len(dims))])
    return level


def normal_values(rng, extent, width, bound, cuts=(), held_as=jnp.bfloat16):
    drawn = jax.random.normal(rng, extent, jnp.float32) * width
    if len(cuts) > 0:
        drawn = steps_of(rng, extent, cuts, -0.22, 0.18) * drawn
    return jnp.clip(drawn, min=-bound, max=bound).astype(held_as)


def setup_inputs(seed: int = 0, part: int = 0) -> dict:
    key_of = jax.random.split(jax.random.key(seed), 6)
    own_keys = jax.random.split(jax.random.fold_in(key_of[5], part), 6)
    return {
        "target_features": draw_target_features(jax.random.fold_in(jax.random.fold_in(key_of[5], part), 71), part),
        "source_features": draw_source_features(jax.random.fold_in(jax.random.fold_in(key_of[5], part), 71), part),
        "vectors": normal_values(own_keys[2], (SOURCES, COLS), 1.0, 6.0, ((0, 16),)),
        "current": normal_values(own_keys[3], (TARGETS, COLS), 1.0, 6.0, ((0, 16),), jnp.float32),
        "previous": draw_previous(jax.random.fold_in(jax.random.fold_in(key_of[5], part), 71), part),
    }


def block_apply(target_rows, source_features, source_sq, vectors, gamma):
    dots = jnp.dot(target_rows, source_features.T, preferred_element_type=jnp.float32)
    scores = 2.0 * gamma * dots - gamma * source_sq[None, :]
    row_max = lax.optimization_barrier(jnp.max(scores, axis=1, keepdims=True))
    weights = jnp.exp(scores - row_max)
    denominator = lax.optimization_barrier(jnp.sum(weights, axis=1, keepdims=True))
    weights_bf = weights.astype(jnp.bfloat16)
    numer = jnp.dot(weights_bf, vectors, preferred_element_type=jnp.float32)
    return numer / denominator

def reference(target_features, source_features, vectors, current, previous):
    gamma = 0.25 / math.sqrt(D)
    source_float = source_features.astype(jnp.float32)
    source_sq = lax.optimization_barrier(jnp.sum(source_float * source_float, axis=1))
    blocks = target_features.reshape(TARGETS // TGT_DEV, TGT_DEV, D)
    applied = lax.map(lambda rows: block_apply(rows, source_features, source_sq, vectors, gamma), blocks)
    applied = applied.reshape(TARGETS, COLS)
    next_iter = 2.0 / 0.05 * (applied - 0.01 * current) - previous
    column_sq = lax.optimization_barrier(jnp.sum(next_iter * next_iter, axis=0))
    return next_iter / jnp.sqrt(column_sq / TARGETS + 1e-06)
```

```python
import functools
import math

import jax
import jax.numpy as jnp
from jax import lax
from jax.experimental import pallas as pl
from jax.experimental.pallas import tpu as pltpu
from jax.sharding import PartitionSpec as P

MESH = pl.DeviceIdType.MESH
CORES = 2
PIECES = 2
TILE = 256
LANES = 128


def folded(mesh):
    line = mesh.devices.reshape(-1, mesh.shape["tgt"])[0][::CORES]
    spots = [getattr(device, "coords", None) for device in line]
    if None in spots or len(spots) % 2:
        return False
    moving = [axis for axis in range(3) if len({spot[axis] for spot in spots}) > 1]
    return len(moving) == 2 and any(len({spot[axis] for spot in spots}) == 2 for axis in moving)


def kernel(
    n, fold, target_hbm, source_hbm, vector_hbm, current_hbm, previous_hbm, result, scale_ref,
    target, current, previous, held, scores, top, column, local_sem, ring_send, ring_recv, pair_send, pair_recv,
    column_send, column_recv,
):
    me = lax.axis_index("tgt")
    chips = n // CORES
    last = chips // 2
    rows, depth = target_hbm.shape
    block = source_hbm.shape[0]
    part = block // PIECES
    gamma = 0.25 / math.sqrt(depth)
    core, chip = me % CORES, me // CORES

    def spot_of(c):
        if not fold:
            return c
        return (c % 2) * (chips - 1) + (c // 2) * (1 - 2 * (c % 2))

    def chip_at(spot):
        if not fold:
            return spot
        side = spot // last
        return (spot + side * (chips - 1 - 2 * spot)) * 2 + side

    spot = spot_of(chip)
    onward = chip_at((spot + chips + 1 - 2 * core) % chips) * CORES + core
    behind = chip_at((spot + chips - 1 + 2 * core) % chips) * CORES + core
    partner = chip * CORES + (1 - core)

    own = [
        pltpu.make_async_copy(source_hbm, held.at[pl.ds(0, block), pl.ds(0, depth)], local_sem.at[0]),
        pltpu.make_async_copy(vector_hbm, held.at[pl.ds(0, block), pl.ds(depth, LANES)], local_sem.at[1]),
    ]
    inputs = [
        pltpu.make_async_copy(target_hbm, target, local_sem.at[2]),
        pltpu.make_async_copy(current_hbm, current, local_sem.at[3]),
        pltpu.make_async_copy(previous_hbm, previous, local_sem.at[4]),
    ]
    for copy in own:
        copy.start()

    barrier = pltpu.get_barrier_semaphore()
    for other in (onward, behind, partner):
        pl.semaphore_signal(barrier, inc=1, device_id={"tgt": other}, device_id_type=MESH)
    pl.semaphore_wait(barrier, 3)

    def first_row(step):
        return 0 if step == 0 else CORES * block * (2 * step - 1)

    def pieces(step):
        return PIECES if step == last else CORES * PIECES

    def place(step, side, piece):
        side = side * (part if step == 0 else pieces(step) * part)
        return held.at[pl.ds(first_row(step) + side + piece * part, part)]

    sent = []

    def ring(step, piece):
        return pltpu.make_async_remote_copy(
            src_ref=place(step - 1, 0, piece),
            dst_ref=place(step, 0, piece),
            send_sem=ring_send.at[step - 1, piece],
            recv_sem=ring_recv.at[step - 1, piece],
            device_id={"tgt": onward},
            device_id_type=MESH,
        )

    def pair(step, piece):
        return pltpu.make_async_remote_copy(
            src_ref=place(step, 0, piece),
            dst_ref=place(step, PIECES if step == 0 else 1, piece),
            send_sem=pair_send.at[step, piece],
            recv_sem=pair_recv.at[step, piece],
            device_id={"tgt": partner},
            device_id_type=MESH,
        )

    def send(copy):
        copy.start()
        sent.append(copy)

    def settle(step):
        for piece in range(pieces(step)):
            pair(step, piece).wait_recv()

    for copy in own:
        copy.wait()
    for piece in range(PIECES):
        send(pair(0, piece))
        send(ring(1, piece))
    for piece in range(PIECES):
        pair(0, piece).wait_recv()
        send(ring(1, PIECES + piece))

    for copy in inputs:
        copy.start()
    top[...] = jnp.full_like(top, -jnp.inf)
    tiles = rows // TILE

    def squares(step):
        width = CORES * block * (2 if 0 < step < last else 1)
        at = pl.ds(first_row(step), width)
        feats = held[at, pl.ds(0, depth)].astype(jnp.float32)
        total = jnp.sum(feats * feats, axis=1, keepdims=True)
        return gamma * jnp.broadcast_to(total, (width, LANES)).T[0:1, :]

    def score(step, offset, low, high, height=TILE):
        width = CORES * block * (2 if 0 < step < last else 1)
        at = pl.ds(first_row(step), width)

        @pl.loop(low, high)
        def _(tile):
            span = pl.ds(pl.multiple_of(tile * height, height), height)
            dots = lax.dot_general(
                target[span, :], held[at, pl.ds(0, depth)], (((1,), (1,)), ((), ())),
                preferred_element_type=jnp.float32,
            )
            value = 2.0 * gamma * dots - offset
            scores[span, at] = value
            most = top[span, :]
            for lane in range(0, width, LANES):
                most = jnp.maximum(most, value[:, lane : lane + LANES])
            top[span, :] = most

    inputs[0].wait()
    score(0, squares(0), 0, tiles)
    for step in range(1, last + 1):
        if step > 1:
            settle(step - 1)
            offset = squares(step - 1)
        count = pieces(step)
        for piece in range(count):
            ring(step, piece).wait_recv()
            if step < last and piece < pieces(step + 1):
                send(ring(step + 1, piece))
            send(pair(step, piece))
            if step > 1:
                score(step - 1, offset, piece * tiles // count, (piece + 1) * tiles // count)
    settle(last)
    score(last, squares(last), 0, 1, rows)

    inputs[1].wait()
    inputs[2].wait()
    group = 2 * TILE

    def finish(tile, total):
        span = pl.ds(pl.multiple_of(tile * group, group), group)
        most = jnp.max(top[span, :], axis=1, keepdims=True)
        weights = jnp.exp(scores[span, :] - most)
        denominator = jnp.sum(weights, axis=1, keepdims=True)
        numer = jnp.dot(
            weights.astype(jnp.bfloat16), held[:, pl.ds(depth, LANES)], preferred_element_type=jnp.float32
        )
        value = 2.0 / 0.05 * (numer / denominator - 0.01 * current[span, :]) - previous[span, :]
        result[span, :] = value
        return total + jnp.sum((value * value).reshape(group // 8, 8, LANES), axis=0)

    total = lax.fori_loop(0, rows // group, finish, jnp.zeros((8, LANES), jnp.float32))
    column[0] = jnp.sum(total, axis=0, keepdims=True)

    gifts = [
        pltpu.make_async_remote_copy(
            src_ref=column.at[0],
            dst_ref=column.at[gap],
            send_sem=column_send.at[gap],
            recv_sem=column_recv.at[gap],
            device_id={"tgt": (me + gap) % n},
            device_id_type=MESH,
        )
        for gap in range(1, n)
    ]
    for copy in gifts:
        copy.start()
    for copy in sent:
        copy.wait_send()
    for copy in gifts:
        copy.wait()
    scale_ref[...] = jnp.sqrt(jnp.sum(column[...], axis=0) / (rows * n) + 1e-06)


def on_device(fold, target_features, source_features, vectors, current, previous):
    n = lax.axis_size("tgt")
    rows, depth = target_features.shape
    block, cols = vectors.shape
    steps = n // CORES // 2 + 1
    next_iter, scale = pl.pallas_call(
        functools.partial(kernel, n, fold),
        out_shape=(
            pltpu.VMEM((rows, cols), jnp.float32),
            pltpu.VMEM((1, cols), jnp.float32),
        ),
        in_specs=[pl.BlockSpec(memory_space=pl.ANY)] * 5,
        out_specs=[pl.BlockSpec(memory_space=pltpu.VMEM)] * 2,
        scratch_shapes=[
            pltpu.VMEM((rows, depth), jnp.bfloat16),
            pltpu.VMEM((rows, cols), jnp.float32),
            pltpu.VMEM((rows, cols), jnp.float32),
            pltpu.VMEM((n * block, depth + cols), jnp.bfloat16),
            pltpu.VMEM((rows, n * block), jnp.float32),
            pltpu.VMEM((rows, LANES), jnp.float32),
            pltpu.VMEM((n, 1, cols), jnp.float32),
            pltpu.SemaphoreType.DMA((5,)),
            pltpu.SemaphoreType.DMA((steps, CORES * PIECES)),
            pltpu.SemaphoreType.DMA((steps, CORES * PIECES)),
            pltpu.SemaphoreType.DMA((steps, CORES * PIECES)),
            pltpu.SemaphoreType.DMA((steps, CORES * PIECES)),
            pltpu.SemaphoreType.DMA((n,)),
            pltpu.SemaphoreType.DMA((n,)),
        ],
        compiler_params=pltpu.CompilerParams(collective_id=0, has_side_effects=True),
    )(target_features, source_features, vectors, current, previous)
    return next_iter / scale


def solution(mesh):
    return jax.shard_map(
        functools.partial(on_device, folded(mesh)),
        mesh=mesh,
        in_specs=(P(("groups", "tgt"), None),) * 5,
        out_specs=P(("groups", "tgt"), None),
        check_vma=False,
    )
```
